32 devices in a mesh: batch: 2 (over x), seq: 4 (over y, core), mp: 4 (over z).
Axes of the slice: x: 2, y: 2, z: 4, core: 2. Of those that a mesh axis runs over, the one named last changes fastest.
Arguments:
- context: bfloat16 [1024, 6144], P(('batch', 'seq'), 'mp'), may hold values from -0.25 to 0.25
- cotangent: bfloat16 [1024, 6144], P(('batch', 'seq'), 'mp'), may hold values from -6 to 6
- out_weight: bfloat16 [6144, 6144], P(None, 'mp'), may hold values from -0.078125 to 0.078125
Outputs:
- grad_weight: float32 [6144, 6144], P(('batch', 'seq'), 'mp')
- grad_context: bfloat16 [1024, 6144], P(('batch', 'seq'), 'mp')
The draws below stay inside these ranges and needn't reach their ends.
All inputs are finite; a program needn't handle non-finite values.
Results may differ from the reference program's by a relative error of at most 0.001.
Values may be sent and summed in bfloat16 or wider, within the bound.
A program may use at most 64 MiB of HBM per device.

```python
import jax
import jax.numpy as jnp
from jax import lax

D = 6144
TOKENS = 1024


def strengthened(values, key, source, target, shards_of, factor):
    def block_of(dim):
        return (jnp.arange(values.shape[dim]) // (values.shape[dim] // shards_of)).reshape((-1,) + (1,) * (values.ndim - 1 - dim))

    near = jax.random.permutation(key, shards_of)[block_of(target)]
    other_side = (block_of(target) + shards_of // 2) % shards_of
    return jnp.where((block_of(source) == near) | (block_of(source) == other_side), factor * values, values)


def block_levels(stream_key, shape, pieces, least, largest):
    def one(dim, parts):
        heights = jax.random.uniform(jax.random.fold_in(jax.random.fold_in(stream_key, 6), dim), (parts,), jnp.float32, least / len(pieces), largest / len(pieces))
        return jnp.repeat(jnp.exp(heights), shape[dim] // parts).reshape((-1,) + (1,) * (len(shape) - dim - 1))

    gain = one(*pieces[0])
    for cut in pieces[1:]:
        gain = gain * one(*cut)
    return gain


def scatter_about(stream_key, dims, scale, limit, split=(), held_as=jnp.bfloat16):
    loudness = block_levels(stream_key, dims, split, -0.22, 0.18) if split else 1.0
    result = jax.random.normal(stream_key, dims, jnp.float32) * scale * loudness
    return jnp.minimum(jnp.maximum(result, -limit), limit).astype(held_as)


def gaussian_with(key, shape, scale, most, pieces, heavy, kind=jnp.bfloat16):
    entries = scale * jax.random.normal(key, shape, jnp.float32)
    if pieces:
        entries = entries * block_levels(key, shape, pieces, -0.22, 0.18)
    return jnp.clip(strengthened(entries, jax.random.fold_in(key, 3), *heavy), -most, most).astype(kind)


def setup_inputs(seed: int = 0) -> dict:
    splits = jax.random.split(jax.random.key(seed), 4)
    return {
        "context": gaussian_with(splits[0], (TOKENS, D), (1 / TOKENS ** 0.5), 0.25, ((0, 8), (1, 4)), (0, 1, 8, 2.0)),
        "cotangent": scatter_about(splits[1], (TOKENS, D), 1.0, 6.0, ((0, 8), (1, 4))),
        "out_weight": scatter_about(splits[2], (D, D), D ** -0.5, 0.078125, ((1, 4),)),
    }


def reference(context, cotangent, out_weight):
    grad_weight = lax.dot_general(context, cotangent, (((0,), (0,)), ((), ())), preferred_element_type=jnp.float32)
    grad_context = lax.dot_general(cotangent, out_weight, (((1,), (1,)), ((), ())), preferred_element_type=jnp.float32)
    return grad_weight, grad_context.astype(jnp.bfloat16)
```

```python
import functools

import jax
import jax.numpy as jnp
from jax import lax
from jax.experimental import pallas as pl
from jax.experimental.pallas import tpu as pltpu
from jax.sharding import PartitionSpec as P

MESH = pl.DeviceIdType.MESH
CHUNKS = 2


def tile_of(width):
    return 256 if width % 256 == 0 else 128


def kernel(
    B, S, M,
    ctx, cot, w, gw, gc,
    zctx, cotall, ctxall, ctxt, part, rup, rdn, wbuf,
    wsem, zr, zu, zd, cs, cr, ks, kf, kr, pus, pds, pur, pdr,
):
    G = B * S
    Q = G // M
    T, width = cot.shape
    rows = T // CHUNKS
    half = S // 2
    b, s, m = lax.axis_index("batch"), lax.axis_index("seq"), lax.axis_index("mp")
    bs = b * S + s
    parity = lax.rem(s, 2)
    partner = (b, s + 1 - 2 * parity, m)
    partner_bs = b * S + s + 1 - 2 * parity
    above, below = (b, s, m + 1), (b, s, m - 1)

    depth = ctxall.shape[2]

    def piece_of(ref, h):
        return ref.at[:, pl.ds(h * depth, depth)] if len(ctx.shape) == 2 else ref.at[h]

    def plane(index):
        return (index // S, lax.rem(index, S), m)

    def remote(src, dst, send, recv, device):
        return pltpu.make_async_remote_copy(
            src_ref=src, dst_ref=dst, send_sem=send, recv_sem=recv,
            device_id=device, device_id_type=MESH,
        )

    order = []
    for step in range((M + 1) // 2):
        order.append(M - 1 - step)
        if step != M - 1 - step:
            order.append(step)

    def load(position):
        k = order[position]
        return pltpu.make_async_copy(
            w.at[pl.ds(k * width, width), :], wbuf.at[position % 2], wsem.at[position % 2]
        )

    load(0).start()
    own_cot = pltpu.make_async_copy(cot, cotall.at[bs], kr.at[bs])
    own_cot.start()

    barrier = pltpu.get_barrier_semaphore()
    for d in range(1, G):
        pl.semaphore_signal(
            barrier, inc=1, device_id=plane(lax.rem(bs + d, G)), device_id_type=MESH
        )

    @pl.when(m > 0)
    def _():
        pl.semaphore_signal(barrier, inc=1, device_id=below, device_id_type=MESH)

    @pl.when(m < M - 1)
    def _():
        pl.semaphore_signal(barrier, inc=1, device_id=above, device_id_type=MESH)

    edge = (m == 0) | (m == M - 1)

    @pl.when(edge)
    def _():
        pl.semaphore_wait(barrier, G)

    @pl.when(jnp.logical_not(edge))
    def _():
        pl.semaphore_wait(barrier, G + 1)

    def ctx_up(src, mm):
        return remote(src, zctx.at[mm], zu.at[mm], zr.at[mm], above)

    def ctx_down(src, mm):
        return remote(src, zctx.at[mm], zd.at[mm], zr.at[mm], below)

    def hand_out(src, mm):
        for h in range(Q):
            dest = mm * Q + h

            @pl.when(dest != bs)
            def _():
                remote(piece_of(src, h), ctxall.at[bs], cs.at[dest], cr.at[bs], plane(dest)).start()

            @pl.when(dest == bs)
            def _():
                pltpu.make_async_copy(piece_of(src, h), ctxall.at[bs], cr.at[bs]).start()

    @pl.when(m < M - 1)
    def _():
        ctx_up(ctx, m).start()

    @pl.when(m > 0)
    def _():
        ctx_down(ctx, m).start()

    def cot_send(dq):
        q = lax.rem(b * half + s // 2 + dq, B * half)
        dest = (q // half, lax.rem(q, half) * 2 + parity, m)
        return remote(cot, cotall.at[bs], ks.at[dq], kr.at[bs], dest)

    def cot_partner():
        return remote(cot, cotall.at[bs], ks.at[0], kr.at[bs], partner)

    def cot_from(dq):
        q = lax.rem(b * half + s // 2 + dq, B * half)
        return (q // half) * S + lax.rem(q, half) * 2 + parity

    def cot_forward(dq):
        j = cot_from(dq)
        return remote(cotall.at[j], cotall.at[j], kf.at[dq], kr.at[j], partner)

    cot_partner().start()
    hand_out(ctx, m)
    for dq in range(1, B * half):
        cot_send(dq).start()

    def chunk(ref, k, c):
        return ref.at[k, pl.ds(c * rows, rows), :]

    def sum_up(k, c):
        return remote(chunk(part, k, c), chunk(rup, k, c), pus.at[k, c], pur.at[k, c], above)

    def sum_down(k, c):
        return remote(chunk(part, k, c), chunk(rdn, k, c), pds.at[k, c], pdr.at[k, c], below)

    span = tile_of(width)

    def product(position):
        k = order[position]
        load(position).wait()
        if position + 1 < M:
            load(position + 1).start()

        @pl.loop(0, width // span)
        def _(t):
            cols = pl.ds(pl.multiple_of(t * span, span), span)
            part[k, :, cols] = lax.dot_general(
                cot[...], wbuf[position % 2, cols, :],
                (((1,), (1,)), ((), ())), preferred_element_type=jnp.float32,
            )

        @pl.when((m == 0) & (k > m))
        def _():
            for c in range(CHUNKS):
                sum_up(k, c).start()

        @pl.when((m == M - 1) & (k < m))
        def _():
            for c in range(CHUNKS):
                sum_down(k, c).start()

    def arrivals(r):
        @pl.when(m >= r)
        def _():
            mm = m - r
            ctx_up(zctx.at[mm], mm).wait_recv()

            @pl.when(m < M - 1)
            def _():
                ctx_up(zctx.at[mm], mm).start()

            hand_out(zctx.at[mm], mm)

        @pl.when(m + r < M)
        def _():
            mm = m + r
            ctx_down(zctx.at[mm], mm).wait_recv()

            @pl.when(m > 0)
            def _():
                ctx_down(zctx.at[mm], mm).start()

            hand_out(zctx.at[mm], mm)

    r = 1
    for position in range(M):
        product(position)
        if position % 2 == 1 and r < M:
            arrivals(r)
            r += 1
    for dq in range(1, B * half):
        j = cot_from(dq)
        remote(cotall.at[j], cotall.at[j], kf.at[dq], kr.at[j], partner).wait_recv()
        cot_forward(dq).start()
    while r < M:
        arrivals(r)
        r += 1

    for j in range(M - 1):
        up, down = M - 1 - j, j

        @pl.when((m > 0) & (m < up))
        def _():
            for c in range(CHUNKS):
                sum_up(up, c).wait_recv()
                piece = pl.ds(c * rows, rows)
                part[up, piece, :] += rup[up, piece, :]
                sum_up(up, c).start()

        @pl.when((m < M - 1) & (m > down))
        def _():
            for c in range(CHUNKS):
                sum_down(down, c).wait_recv()
                piece = pl.ds(c * rows, rows)
                part[down, piece, :] += rdn[down, piece, :]
                sum_down(down, c).start()

    own_cot.wait()
    for d in range(1, G):
        j = lax.rem(bs + d, G)
        remote(ctxall.at[j], ctxall.at[j], cs.at[j], cr.at[j], partner).wait_recv()
    pltpu.make_async_copy(ctxall.at[bs], ctxall.at[bs], cr.at[bs]).wait()
    remote(cotall.at[partner_bs], cotall.at[partner_bs], ks.at[0], kr.at[partner_bs], partner).wait_recv()
    for dq in range(1, B * half):
        j = cot_from(dq) + 1 - 2 * parity
        remote(cotall.at[j], cotall.at[j], kf.at[dq], kr.at[j], partner).wait_recv()

    for j in range(G):
        ctxt[:, j * T : (j + 1) * T] = ctxall[j].T
    gspan = tile_of(width)

    @pl.loop(0, width // gspan)
    def _(t):
        cols = pl.ds(pl.multiple_of(t * gspan, gspan), gspan)
        gw[:, cols] = jnp.dot(
            ctxt[...], cotall[:, :, cols].reshape(G * T, gspan),
            preferred_element_type=jnp.float32,
        )

    for c in range(CHUNKS):
        piece = pl.ds(c * rows, rows)

        @pl.when(m > 0)
        def _():
            sum_up(m, c).wait_recv()
            part[m, piece, :] += rup[m, piece, :]

        @pl.when(m < M - 1)
        def _():
            sum_down(m, c).wait_recv()
            part[m, piece, :] += rdn[m, piece, :]

        gc[piece, :] = part[m, piece, :].astype(gc.dtype)

    for mm in range(M):
        @pl.when((m < M - 1) & (mm <= m))
        def _():
            ctx_up(ctx, mm).wait_send()

        @pl.when((m > 0) & (mm >= m))
        def _():
            ctx_down(ctx, mm).wait_send()

        for c in range(CHUNKS):
            @pl.when(mm > m)
            def _():
                sum_up(mm, c).wait_send()

            @pl.when(mm < m)
            def _():
                sum_down(mm, c).wait_send()

    for dest in range(G):
        @pl.when(dest != bs)
        def _():
            remote(piece_of(ctx, 0), ctxall.at[bs], cs.at[dest], cr.at[bs], partner).wait_send()

    cot_partner().wait_send()
    for dq in range(1, B * half):
        cot_send(dq).wait_send()
        cot_forward(dq).wait_send()


def shards(context, cotangent, out_weight):
    B, S, M = lax.axis_size("batch"), lax.axis_size("seq"), lax.axis_size("mp")
    G = B * S
    T, width = cotangent.shape
    Q = G // M
    F = context.shape[1] // Q
    pieces = context
    if F % 128:
        pieces = jnp.stack([context[:, h * F : (h + 1) * F] for h in range(Q)])
    pairs = B * (S // 2)
    dma = pltpu.SemaphoreType.DMA
    vmem = pl.BlockSpec(memory_space=pltpu.VMEM)
    return pl.pallas_call(
        functools.partial(kernel, B, S, M),
        out_shape=(
            jax.ShapeDtypeStruct((F, width), jnp.float32),
            jax.ShapeDtypeStruct((T, context.shape[1]), jnp.bfloat16),
        ),
        in_specs=[vmem, vmem, pl.BlockSpec(memory_space=pl.ANY)],
        out_specs=(vmem, vmem),
        scratch_shapes=[
            pltpu.VMEM((M, *pieces.shape), jnp.bfloat16),
            pltpu.VMEM((G, T, width), jnp.bfloat16),
            pltpu.VMEM((G, T, F), jnp.bfloat16),
            pltpu.VMEM((F, G * T), jnp.bfloat16),
            pltpu.VMEM((M, T, width), jnp.float32),
            pltpu.VMEM((M, T, width), jnp.float32),
            pltpu.VMEM((M, T, width), jnp.float32),
            pltpu.VMEM((2, width, width), jnp.bfloat16),
            dma((2,)), dma((M,)), dma((M,)), dma((M,)),
            dma((G,)), dma((G,)), dma((pairs,)), dma((pairs,)), dma((G,)),
            dma((M, CHUNKS)), dma((M, CHUNKS)), dma((M, CHUNKS)), dma((M, CHUNKS)),
        ],
        compiler_params=pltpu.CompilerParams(collective_id=0, has_side_effects=True),
        name="output_projection_backward",
    )(pieces, cotangent, out_weight)


def solution(mesh):
    return jax.shard_map(
        shards,
        mesh=mesh,
        in_specs=(P(("batch", "seq"), "mp"), P(("batch", "seq"), "mp"), P(None, "mp")),
        out_specs=(P(("batch", "seq"), "mp"), P(("batch", "seq"), "mp")),
        check_vma=False,
    )
```

```python
import functools

import jax
import jax.numpy as jnp
from jax import lax
from jax.experimental import pallas as pl
from jax.experimental.pallas import tpu as pltpu
from jax.sharding import PartitionSpec as P

MESH = pl.DeviceIdType.MESH
CHUNKS = 2


def tile_of(width):
    return 256 if width % 256 == 0 else 128


def kernel(
    B, S, M,
    ctx, cot, w, gw, gc,
    zctx, cotall, ctxall, ctxt, part, rup, rdn, wbuf,
    wsem, zr, zu, zd, cs, cr, ks, kf, kr, pus, pds, pur, pdr,
):
    G = B * S
    Q = G // M
    T, width = cot.shape
    rows = T // CHUNKS
    half = S // 2
    b, s, m = lax.axis_index("batch"), lax.axis_index("seq"), lax.axis_index("mp")
    bs = b * S + s
    parity = lax.rem(s, 2)
    partner = (b, s + 1 - 2 * parity, m)
    partner_bs = b * S + s + 1 - 2 * parity
    above, below = (b, s, m + 1), (b, s, m - 1)

    depth = ctxall.shape[2]

    def piece_of(ref, h):
        return ref.at[:, pl.ds(h * depth, depth)] if len(ctx.shape) == 2 else ref.at[h]

    def plane(index):
        return (index // S, lax.rem(index, S), m)

    def remote(src, dst, send, recv, device):
        return pltpu.make_async_remote_copy(
            src_ref=src, dst_ref=dst, send_sem=send, recv_sem=recv,
            device_id=device, device_id_type=MESH,
        )

    low = 2 * m < M

    def target(position):
        return jnp.where(low, M - 1 - position, position)

    def load(position):
        k = target(position)
        return pltpu.make_async_copy(
            w.at[pl.ds(k * width, width), :], wbuf.at[position % 2], wsem.at[position % 2]
        )

    load(0).start()
    own_cot = pltpu.make_async_copy(cot, cotall.at[bs], kr.at[bs])
    own_cot.start()

    barrier = pltpu.get_barrier_semaphore()
    for d in range(1, G):
        pl.semaphore_signal(
            barrier, inc=1, device_id=plane(lax.rem(bs + d, G)), device_id_type=MESH
        )

    @pl.when(m > 0)
    def _():
        pl.semaphore_signal(barrier, inc=1, device_id=below, device_id_type=MESH)

    @pl.when(m < M - 1)
    def _():
        pl.semaphore_signal(barrier, inc=1, device_id=above, device_id_type=MESH)

    edge = (m == 0) | (m == M - 1)

    @pl.when(edge)
    def _():
        pl.semaphore_wait(barrier, G)

    @pl.when(jnp.logical_not(edge))
    def _():
        pl.semaphore_wait(barrier, G + 1)

    def ctx_up(src, mm):
        return remote(src, zctx.at[mm], zu.at[mm], zr.at[mm], above)

    def ctx_down(src, mm):
        return remote(src, zctx.at[mm], zd.at[mm], zr.at[mm], below)

    def hand_out(src, mm):
        for h in range(Q):
            dest = mm * Q + h

            @pl.when(dest != bs)
            def _():
                remote(piece_of(src, h), ctxall.at[bs], cs.at[dest], cr.at[bs], plane(dest)).start()

            @pl.when(dest == bs)
            def _():
                pltpu.make_async_copy(piece_of(src, h), ctxall.at[bs], cr.at[bs]).start()

    @pl.when(m < M - 1)
    def _():
        ctx_up(ctx, m).start()

    @pl.when(m > 0)
    def _():
        ctx_down(ctx, m).start()

    def cot_send(dq):
        q = lax.rem(b * half + s // 2 + dq, B * half)
        dest = (q // half, lax.rem(q, half) * 2 + parity, m)
        return remote(cot, cotall.at[bs], ks.at[dq], kr.at[bs], dest)

    def cot_partner():
        return remote(cot, cotall.at[bs], ks.at[0], kr.at[bs], partner)

    def cot_from(dq):
        q = lax.rem(b * half + s // 2 + dq, B * half)
        return (q // half) * S + lax.rem(q, half) * 2 + parity

    def cot_forward(dq):
        j = cot_from(dq)
        return remote(cotall.at[j], cotall.at[j], kf.at[dq], kr.at[j], partner)

    cot_partner().start()
    for dq in range(1, B * half):
        cot_send(dq).start()
    hand_out(ctx, m)

    def chunk(ref, k, c):
        return ref.at[k, pl.ds(c * rows, rows), :]

    def sum_up(k, c):
        return remote(chunk(part, k, c), chunk(rup, k, c), pus.at[k, c], pur.at[k, c], above)

    def sum_down(k, c):
        return remote(chunk(part, k, c), chunk(rdn, k, c), pds.at[k, c], pdr.at[k, c], below)

    span = tile_of(width)

    def product(position):
        k = target(position)
        load(position).wait()
        if position + 1 < M:
            load(position + 1).start()

        @pl.loop(0, width // span)
        def _(t):
            cols = pl.ds(pl.multiple_of(t * span, span), span)
            part[k, :, cols] = lax.dot_general(
                cot[...], wbuf[position % 2, cols, :],
                (((1,), (1,)), ((), ())), preferred_element_type=jnp.float32,
            )

        @pl.when((m == 0) & (k > m))
        def _():
            for c in range(CHUNKS):
                sum_up(k, c).start()

        @pl.when((m == M - 1) & (k < m))
        def _():
            for c in range(CHUNKS):
                sum_down(k, c).start()

    def arrivals(r):
        @pl.when(m >= r)
        def _():
            mm = m - r
            ctx_up(zctx.at[mm], mm).wait_recv()

            @pl.when(m < M - 1)
            def _():
                ctx_up(zctx.at[mm], mm).start()

            hand_out(zctx.at[mm], mm)

        @pl.when(m + r < M)
        def _():
            mm = m + r
            ctx_down(zctx.at[mm], mm).wait_recv()

            @pl.when(m > 0)
            def _():
                ctx_down(zctx.at[mm], mm).start()

            hand_out(zctx.at[mm], mm)

    def pass_up(k, c):
        piece = pl.ds(c * rows, rows)
        sum_up(k, c).wait_recv()
        part[k, piece, :] += rup[k, piece, :]
        sum_up(k, c).start()

    def pass_down(k, c):
        piece = pl.ds(c * rows, rows)
        sum_down(k, c).wait_recv()
        part[k, piece, :] += rdn[k, piece, :]
        sum_down(k, c).start()

    def chain(tick):
        up = M - 1 - (tick - m)
        down = tick - (M - 1 - m)
        for c in range(CHUNKS):
            @pl.when((m > 0) & (m < up) & (up < M))
            def _():
                pass_up(up, c)

            @pl.when((m < M - 1) & (m > down) & (down >= 0))
            def _():
                pass_down(down, c)

    r = 1
    for position in range(M):
        product(position)
        if position % 2 == 1 and r < M:
            arrivals(r)
            r += 1
    if M > 2:
        chain(1)
    for dq in range(1, B * half):
        j = cot_from(dq)
        remote(cotall.at[j], cotall.at[j], kf.at[dq], kr.at[j], partner).wait_recv()
        cot_forward(dq).start()
    while r < M:
        arrivals(r)
        r += 1
    for tick in range(2, M - 1):
        chain(tick)

    own_cot.wait()
    for d in range(1, G):
        j = lax.rem(bs + d, G)
        remote(ctxall.at[j], ctxall.at[j], cs.at[j], cr.at[j], partner).wait_recv()
    pltpu.make_async_copy(ctxall.at[bs], ctxall.at[bs], cr.at[bs]).wait()
    remote(cotall.at[partner_bs], cotall.at[partner_bs], ks.at[0], kr.at[partner_bs], partner).wait_recv()
    for dq in range(1, B * half):
        j = cot_from(dq) + 1 - 2 * parity
        remote(cotall.at[j], cotall.at[j], kf.at[dq], kr.at[j], partner).wait_recv()

    for j in range(G):
        ctxt[:, j * T : (j + 1) * T] = ctxall[j].T
    gspan = tile_of(width)

    @pl.loop(0, width // gspan)
    def _(t):
        cols = pl.ds(pl.multiple_of(t * gspan, gspan), gspan)
        gw[:, cols] = jnp.dot(
            ctxt[...], cotall[:, :, cols].reshape(G * T, gspan),
            preferred_element_type=jnp.float32,
        )

    for c in range(CHUNKS):
        piece = pl.ds(c * rows, rows)

        @pl.when(m > 0)
        def _():
            sum_up(m, c).wait_recv()
            part[m, piece, :] += rup[m, piece, :]

        @pl.when(m < M - 1)
        def _():
            sum_down(m, c).wait_recv()
            part[m, piece, :] += rdn[m, piece, :]

        gc[piece, :] = part[m, piece, :].astype(gc.dtype)

    for mm in range(M):
        @pl.when((m < M - 1) & (mm <= m))
        def _():
            ctx_up(ctx, mm).wait_send()

        @pl.when((m > 0) & (mm >= m))
        def _():
            ctx_down(ctx, mm).wait_send()

        for c in range(CHUNKS):
            @pl.when(mm > m)
            def _():
                sum_up(mm, c).wait_send()

            @pl.when(mm < m)
            def _():
                sum_down(mm, c).wait_send()

    for dest in range(G):
        @pl.when(dest != bs)
        def _():
            remote(piece_of(ctx, 0), ctxall.at[bs], cs.at[dest], cr.at[bs], partner).wait_send()

    cot_partner().wait_send()
    for dq in range(1, B * half):
        cot_send(dq).wait_send()
        cot_forward(dq).wait_send()


def shards(context, cotangent, out_weight):
    B, S, M = lax.axis_size("batch"), lax.axis_size("seq"), lax.axis_size("mp")
    G = B * S
    T, width = cotangent.shape
    Q = G // M
    F = context.shape[1] // Q
    pieces = context
    if F % 128:
        pieces = jnp.stack([context[:, h * F : (h + 1) * F] for h in range(Q)])
    pairs = B * (S // 2)
    dma = pltpu.SemaphoreType.DMA
    vmem = pl.BlockSpec(memory_space=pltpu.VMEM)
    return pl.pallas_call(
        functools.partial(kernel, B, S, M),
        out_shape=(
            jax.ShapeDtypeStruct((F, width), jnp.float32),
            jax.ShapeDtypeStruct((T, context.shape[1]), jnp.bfloat16),
        ),
        in_specs=[vmem, vmem, pl.BlockSpec(memory_space=pl.ANY)],
        out_specs=(vmem, vmem),
        scratch_shapes=[
            pltpu.VMEM((M, *pieces.shape), jnp.bfloat16),
            pltpu.VMEM((G, T, width), jnp.bfloat16),
            pltpu.VMEM((G, T, F), jnp.bfloat16),
            pltpu.VMEM((F, G * T), jnp.bfloat16),
            pltpu.VMEM((M, T, width), jnp.float32),
            pltpu.VMEM((M, T, width), jnp.float32),
            pltpu.VMEM((M, T, width), jnp.float32),
            pltpu.VMEM((2, width, width), jnp.bfloat16),
            dma((2,)), dma((M,)), dma((M,)), dma((M,)),
            dma((G,)), dma((G,)), dma((pairs,)), dma((pairs,)), dma((G,)),
            dma((M, CHUNKS)), dma((M, CHUNKS)), dma((M, CHUNKS)), dma((M, CHUNKS)),
        ],
        compiler_params=pltpu.CompilerParams(collective_id=0, has_side_effects=True),
        name="output_projection_backward",
    )(pieces, cotangent, out_weight)


def solution(mesh):
    return jax.shard_map(
        shards,
        mesh=mesh,
        in_specs=(P(("batch", "seq"), "mp"), P(("batch", "seq"), "mp"), P(None, "mp")),
        out_specs=(P(("batch", "seq"), "mp"), P(("batch", "seq"), "mp")),
        check_vma=False,
    )
```

```python
import functools

import jax
import jax.numpy as jnp
from jax import lax
from jax.experimental import pallas as pl
from jax.experimental.pallas import tpu as pltpu
from jax.sharding import PartitionSpec as P

MESH = pl.DeviceIdType.MESH
CHUNKS = 2


def tile_of(width):
    return 256 if width % 256 == 0 else 128


def kernel(
    B, S, M,
    ctx, cot, w, gw, gc,
    zctx, cotall, ctxall, ctxt, part, rup, rdn, wbuf,
    wsem, zr, zu, zd, cs, cr, ks, kf, kr, pus, pds, pur, pdr,
):
    G = B * S
    Q = G // M
    T, width = cot.shape
    rows = T // CHUNKS
    half = S // 2
    b, s, m = lax.axis_index("batch"), lax.axis_index("seq"), lax.axis_index("mp")
    bs = b * S + s
    parity = lax.rem(s, 2)
    partner = (b, s + 1 - 2 * parity, m)
    partner_bs = b * S + s + 1 - 2 * parity
    above, below = (b, s, m + 1), (b, s, m - 1)

    depth = ctxall.shape[2]

    def piece_of(ref, h):
        return ref.at[:, pl.ds(h * depth, depth)] if len(ctx.shape) == 2 else ref.at[h]

    def plane(index):
        return (index // S, lax.rem(index, S), m)

    def remote(src, dst, send, recv, device):
        return pltpu.make_async_remote_copy(
            src_ref=src, dst_ref=dst, send_sem=send, recv_sem=recv,
            device_id=device, device_id_type=MESH,
        )

    low = 2 * m < M

    def target(position):
        return jnp.where(low, M - 1 - position, position)

    def load(position):
        k = target(position)
        return pltpu.make_async_copy(
            w.at[pl.ds(k * width, width), :], wbuf.at[position % 2], wsem.at[position % 2]
        )

    load(0).start()
    own_cot = pltpu.make_async_copy(cot, cotall.at[bs], kr.at[bs])
    own_cot.start()

    barrier = pltpu.get_barrier_semaphore()
    for d in range(1, G):
        pl.semaphore_signal(
            barrier, inc=1, device_id=plane(lax.rem(bs + d, G)), device_id_type=MESH
        )

    @pl.when(m > 0)
    def _():
        pl.semaphore_signal(barrier, inc=1, device_id=below, device_id_type=MESH)

    @pl.when(m < M - 1)
    def _():
        pl.semaphore_signal(barrier, inc=1, device_id=above, device_id_type=MESH)

    edge = (m == 0) | (m == M - 1)

    @pl.when(edge)
    def _():
        pl.semaphore_wait(barrier, G)

    @pl.when(jnp.logical_not(edge))
    def _():
        pl.semaphore_wait(barrier, G + 1)

    def ctx_up(src, mm):
        return remote(src, zctx.at[mm], zu.at[mm], zr.at[mm], above)

    def ctx_down(src, mm):
        return remote(src, zctx.at[mm], zd.at[mm], zr.at[mm], below)

    def hand_out(src, mm):
        for h in range(Q):
            dest = mm * Q + h

            @pl.when(dest != bs)
            def _():
                remote(piece_of(src, h), ctxall.at[bs], cs.at[dest], cr.at[bs], plane(dest)).start()

            @pl.when(dest == bs)
            def _():
                pltpu.make_async_copy(piece_of(src, h), ctxall.at[bs], cr.at[bs]).start()

    @pl.when(m < M - 1)
    def _():
        ctx_up(ctx, m).start()

    @pl.when(m > 0)
    def _():
        ctx_down(ctx, m).start()

    def cot_send(dq):
        q = lax.rem(b * half + s // 2 + dq, B * half)
        dest = (q // half, lax.rem(q, half) * 2 + parity, m)
        return remote(cot, cotall.at[bs], ks.at[dq], kr.at[bs], dest)

    def cot_partner():
        return remote(cot, cotall.at[bs], ks.at[0], kr.at[bs], partner)

    def cot_from(dq):
        q = lax.rem(b * half + s // 2 + dq, B * half)
        return (q // half) * S + lax.rem(q, half) * 2 + parity

    def cot_forward(dq):
        j = cot_from(dq)
        return remote(cotall.at[j], cotall.at[j], kf.at[dq], kr.at[j], partner)

    cot_partner().start()
    for dq in range(1, B * half):
        cot_send(dq).start()
    hand_out(ctx, m)

    def chunk(ref, k, c):
        return ref.at[k, pl.ds(c * rows, rows), :]

    def sum_up(k, c):
        return remote(chunk(part, k, c), chunk(rup, k, c), pus.at[k, c], pur.at[k, c], above)

    def sum_down(k, c):
        return remote(chunk(part, k, c), chunk(rdn, k, c), pds.at[k, c], pdr.at[k, c], below)

    span = tile_of(width)

    def product(position):
        k = target(position)
        load(position).wait()
        if position + 1 < M:
            load(position + 1).start()

        @pl.loop(0, width // span)
        def _(t):
            cols = pl.ds(pl.multiple_of(t * span, span), span)
            part[k, :, cols] = lax.dot_general(
                cot[...], wbuf[position % 2, cols, :],
                (((1,), (1,)), ((), ())), preferred_element_type=jnp.float32,
            )

        @pl.when((m == 0) & (k > m))
        def _():
            for c in range(CHUNKS):
                sum_up(k, c).start()

        @pl.when((m == M - 1) & (k < m))
        def _():
            for c in range(CHUNKS):
                sum_down(k, c).start()

    def arrivals(r):
        @pl.when(m >= r)
        def _():
            mm = m - r
            ctx_up(zctx.at[mm], mm).wait_recv()

            @pl.when(m < M - 1)
            def _():
                ctx_up(zctx.at[mm], mm).start()

            hand_out(zctx.at[mm], mm)

        @pl.when(m + r < M)
        def _():
            mm = m + r
            ctx_down(zctx.at[mm], mm).wait_recv()

            @pl.when(m > 0)
            def _():
                ctx_down(zctx.at[mm], mm).start()

            hand_out(zctx.at[mm], mm)

    def pass_up(k, c):
        piece = pl.ds(c * rows, rows)
        sum_up(k, c).wait_recv()
        part[k, piece, :] += rup[k, piece, :]
        sum_up(k, c).start()

    def pass_down(k, c):
        piece = pl.ds(c * rows, rows)
        sum_down(k, c).wait_recv()
        part[k, piece, :] += rdn[k, piece, :]
        sum_down(k, c).start()

    def chain(tick):
        up = M - 1 - (tick - m)
        down = tick - (M - 1 - m)
        for c in range(CHUNKS):
            @pl.when((m > 0) & (m < up) & (up < M))
            def _():
                pass_up(up, c)

            @pl.when((m < M - 1) & (m > down) & (down >= 0))
            def _():
                pass_down(down, c)

    r = 1
    for position in range(M):
        product(position)
        if position % 2 == 1 and r < M:
            arrivals(r)
            r += 1
    if M > 2:
        chain(1)
    for dq in range(1, B * half):
        j = cot_from(dq)
        remote(cotall.at[j], cotall.at[j], kf.at[dq], kr.at[j], partner).wait_recv()
        cot_forward(dq).start()
    while r < M:
        arrivals(r)
        r += 1
    for tick in range(2, M - 1):
        chain(tick)

    own_cot.wait()
    for d in range(1, G):
        j = lax.rem(bs + d, G)
        remote(ctxall.at[j], ctxall.at[j], cs.at[j], cr.at[j], partner).wait_recv()
    pltpu.make_async_copy(ctxall.at[bs], ctxall.at[bs], cr.at[bs]).wait()
    remote(cotall.at[partner_bs], cotall.at[partner_bs], ks.at[0], kr.at[partner_bs], partner).wait_recv()
    for dq in range(1, B * half):
        j = cot_from(dq) + 1 - 2 * parity
        remote(cotall.at[j], cotall.at[j], kf.at[dq], kr.at[j], partner).wait_recv()

    for j in range(G):
        ctxt[:, j * T : (j + 1) * T] = ctxall[j].T
    gspan = tile_of(width)

    @pl.loop(0, width // gspan)
    def _(t):
        cols = pl.ds(pl.multiple_of(t * gspan, gspan), gspan)
        gw[:, cols] = jnp.dot(
            ctxt[...], cotall[:, :, cols].reshape(G * T, gspan),
            preferred_element_type=jnp.float32,
        )

    for c in range(CHUNKS):
        piece = pl.ds(c * rows, rows)

        @pl.when(m > 0)
        def _():
            sum_up(m, c).wait_recv()
            part[m, piece, :] += rup[m, piece, :]

        @pl.when(m < M - 1)
        def _():
            sum_down(m, c).wait_recv()
            part[m, piece, :] += rdn[m, piece, :]

        gc[piece, :] = part[m, piece, :].astype(gc.dtype)

    for mm in range(M):
        @pl.when((m < M - 1) & (mm <= m))
        def _():
            ctx_up(ctx, mm).wait_send()

        @pl.when((m > 0) & (mm >= m))
        def _():
            ctx_down(ctx, mm).wait_send()

        for c in range(CHUNKS):
            @pl.when(mm > m)
            def _():
                sum_up(mm, c).wait_send()

            @pl.when(mm < m)
            def _():
                sum_down(mm, c).wait_send()

    for dest in range(G):
        @pl.when(dest != bs)
        def _():
            remote(piece_of(ctx, 0), ctxall.at[bs], cs.at[dest], cr.at[bs], partner).wait_send()

    cot_partner().wait_send()
    for dq in range(1, B * half):
        cot_send(dq).wait_send()
        cot_forward(dq).wait_send()


def shards(context, cotangent, out_weight):
    B, S, M = lax.axis_size("batch"), lax.axis_size("seq"), lax.axis_size("mp")
    G = B * S
    T, width = cotangent.shape
    Q = G // M
    F = context.shape[1] // Q
    pieces = context
    if F % 128:
        pieces = jnp.stack([context[:, h * F : (h + 1) * F] for h in range(Q)])
    pairs = B * (S // 2)
    dma = pltpu.SemaphoreType.DMA
    vmem = pl.BlockSpec(memory_space=pltpu.VMEM)
    return pl.pallas_call(
        functools.partial(kernel, B, S, M),
        out_shape=(
            jax.ShapeDtypeStruct((F, width), jnp.float32),
            jax.ShapeDtypeStruct((T, context.shape[1]), jnp.bfloat16),
        ),
        in_specs=[vmem, vmem, pl.BlockSpec(memory_space=pl.ANY)],
        out_specs=(vmem, vmem),
        scratch_shapes=[
            pltpu.VMEM((M, *pieces.shape), jnp.bfloat16),
            pltpu.VMEM((G, T, width), jnp.bfloat16),
            pltpu.VMEM((G, T, F), jnp.bfloat16),
            pltpu.VMEM((F, G * T), jnp.bfloat16),
            pltpu.VMEM((M, T, width), jnp.float32),
            pltpu.VMEM((M, T, width), jnp.float32),
            pltpu.VMEM((M, T, width), jnp.float32),
            pltpu.VMEM((2, width, width), jnp.bfloat16),
            dma((2,)), dma((M,)), dma((M,)), dma((M,)),
            dma((G,)), dma((G,)), dma((pairs,)), dma((pairs,)), dma((G,)),
            dma((M, CHUNKS)), dma((M, CHUNKS)), dma((M, CHUNKS)), dma((M, CHUNKS)),
        ],
        compiler_params=pltpu.CompilerParams(collective_id=0, has_side_effects=True, vmem_limit_bytes=44 * 1024 * 1024),
        name="output_projection_backward",
    )(pieces, cotangent, out_weight)


def solution(mesh):
    return jax.shard_map(
        shards,
        mesh=mesh,
        in_specs=(P(("batch", "seq"), "mp"), P(("batch", "seq"), "mp"), P(None, "mp")),
        out_specs=(P(("batch", "seq"), "mp"), P(("batch", "seq"), "mp")),
        check_vma=False,
    )
```

```python
import functools

import jax
import jax.numpy as jnp
from jax import lax
from jax.experimental import pallas as pl
from jax.experimental.pallas import tpu as pltpu
from jax.sharding import PartitionSpec as P

MESH = pl.DeviceIdType.MESH
CHUNKS = 2
PARTS = 4
LEVELS = 36
BASE = 75


def tile_of(width):
    return 256 if width % 256 == 0 else 128


def kernel(
    B, S, M,
    ctx, cot, w, gw, gc,
    zctx, cotall, ctxall, ctxt, part, rup, rdn, high, low_bits, hup, lup, hdn, ldn, wbuf,
    wsem, zr, zu, zd, cs, cr, ks, kf, kr, pus, pds, pur, pdr,
):
    G = B * S
    Q = G // M
    T, width = cot.shape
    rows = T // CHUNKS
    half = S // 2
    b, s, m = lax.axis_index("batch"), lax.axis_index("seq"), lax.axis_index("mp")
    bs = b * S + s
    parity = lax.rem(s, 2)
    partner = (b, s + 1 - 2 * parity, m)
    partner_bs = b * S + s + 1 - 2 * parity
    above, below = (b, s, m + 1), (b, s, m - 1)

    depth = ctxall.shape[2]

    def piece_of(ref, h):
        return ref.at[:, pl.ds(h * depth, depth)] if len(ctx.shape) == 2 else ref.at[h]

    def plane(index):
        return (index // S, lax.rem(index, S), m)

    def remote(src, dst, send, recv, device):
        return pltpu.make_async_remote_copy(
            src_ref=src, dst_ref=dst, send_sem=send, recv_sem=recv,
            device_id=device, device_id_type=MESH,
        )

    low = 2 * m < M

    def target(position):
        return jnp.where(low, M - 1 - position, position)

    def load(position):
        k = target(position)
        return pltpu.make_async_copy(
            w.at[pl.ds(k * width, width), :], wbuf.at[position % 2], wsem.at[position % 2]
        )

    load(0).start()
    own_cot = pltpu.make_async_copy(cot, cotall.at[bs], kr.at[bs])
    own_cot.start()

    barrier = pltpu.get_barrier_semaphore()
    for d in range(1, G):
        pl.semaphore_signal(
            barrier, inc=1, device_id=plane(lax.rem(bs + d, G)), device_id_type=MESH
        )

    @pl.when(m > 0)
    def _():
        pl.semaphore_signal(barrier, inc=1, device_id=below, device_id_type=MESH)

    @pl.when(m < M - 1)
    def _():
        pl.semaphore_signal(barrier, inc=1, device_id=above, device_id_type=MESH)

    edge = (m == 0) | (m == M - 1)

    @pl.when(edge)
    def _():
        pl.semaphore_wait(barrier, G)

    @pl.when(jnp.logical_not(edge))
    def _():
        pl.semaphore_wait(barrier, G + 1)

    def ctx_up(src, mm):
        return remote(src, zctx.at[mm], zu.at[mm], zr.at[mm], above)

    def ctx_down(src, mm):
        return remote(src, zctx.at[mm], zd.at[mm], zr.at[mm], below)

    def hand_out(src, mm):
        for h in range(Q):
            dest = mm * Q + h

            @pl.when(dest != bs)
            def _():
                remote(piece_of(src, h), ctxall.at[bs], cs.at[dest], cr.at[bs], plane(dest)).start()

            @pl.when(dest == bs)
            def _():
                pltpu.make_async_copy(piece_of(src, h), ctxall.at[bs], cr.at[bs]).start()

    @pl.when(m < M - 1)
    def _():
        ctx_up(ctx, m).start()

    @pl.when(m > 0)
    def _():
        ctx_down(ctx, m).start()

    def cot_send(dq):
        q = lax.rem(b * half + s // 2 + dq, B * half)
        dest = (q // half, lax.rem(q, half) * 2 + parity, m)
        return remote(cot, cotall.at[bs], ks.at[dq], kr.at[bs], dest)

    def cot_partner():
        return remote(cot, cotall.at[bs], ks.at[0], kr.at[bs], partner)

    def cot_from(dq):
        q = lax.rem(b * half + s // 2 + dq, B * half)
        return (q // half) * S + lax.rem(q, half) * 2 + parity

    def cot_forward(dq):
        j = cot_from(dq)
        return remote(cotall.at[j], cotall.at[j], kf.at[dq], kr.at[j], partner)

    cot_partner().start()
    for dq in range(1, B * half):
        cot_send(dq).start()
    hand_out(ctx, m)

    def chunk(ref, k, c):
        return ref.at[k, pl.ds(c * rows, rows), :]

    quarter = rows // PARTS
    ups = (above, pus, pur, rup, hup, lup)
    downs = (below, pds, pdr, rdn, hdn, ldn)

    def short(ref, k, c):
        return ref.at[k, pl.ds(c * quarter, quarter), :]

    def plain(way, k, c):
        device, send, recv, full, _, _ = way
        return remote(chunk(part, k, c), chunk(full, k, c), send.at[k, c, 0], recv.at[k, c, 0], device)

    def coded(way, k, c):
        device, send, recv, _, rhigh, rlow = way
        return (
            remote(chunk(high, k, c), chunk(rhigh, k, c), send.at[k, c, 0], recv.at[k, c, 0], device),
            remote(short(low_bits, k, c), short(rlow, k, c), send.at[k, c, 1], recv.at[k, c, 1], device),
        )

    def is_coded(way, sender, k):
        if way is ups:
            return (sender == 0) | ((k == M - 1) & (sender < M - 2))
        return (sender == M - 1) | ((k == 0) & (sender > 1))

    def encode(k, c):
        @pl.loop(0, width // span)
        def _(t):
            cols = pl.ds(pl.multiple_of(t * span, span), span)
            total = None
            for i in range(PARTS):
                lines = pl.ds(c * rows + i * quarter, quarter)
                value = part[k, lines, cols]
                top = value.astype(jnp.bfloat16)
                high[k, lines, cols] = top
                top = top.astype(jnp.float32)
                size = jnp.abs(top)
                usable = size > 1e-30
                scale = (256.0 * LEVELS) / jnp.where(usable, size, 1.0)
                rest = jnp.floor(jnp.where(usable, (value - top) * scale, 0.0) + 0.5)
                total = rest if total is None else total * BASE + rest
            low_bits[k, pl.ds(c * quarter, quarter), cols] = total

    def decode(rhigh, rlow, k, c):
        @pl.loop(0, width // span)
        def _(t):
            cols = pl.ds(pl.multiple_of(t * span, span), span)
            left = rlow[k, pl.ds(c * quarter, quarter), cols]
            for i in range(PARTS):
                lines = pl.ds(c * rows + i * quarter, quarter)
                unit = float(BASE ** (PARTS - 1 - i))
                rest = jnp.floor(left * (1.0 / unit) + 0.5)
                left = left - rest * unit
                top = rhigh[k, lines, cols].astype(jnp.float32)
                value = top + rest * (jnp.abs(top) * (1.0 / (256.0 * LEVELS)))
                part[k, lines, cols] += value

    def send_sum(way, k, c):
        code = is_coded(way, m, k)

        @pl.when(code)
        def _():
            encode(k, c)
            for copy in coded(way, k, c):
                copy.start()

        @pl.when(jnp.logical_not(code))
        def _():
            plain(way, k, c).start()

    def sent_sum(way, k, c):
        code = is_coded(way, m, k)

        @pl.when(code)
        def _():
            for copy in coded(way, k, c):
                copy.wait_send()

        @pl.when(jnp.logical_not(code))
        def _():
            plain(way, k, c).wait_send()

    def take_sum(way, k, c):
        code = is_coded(way, m - 1 if way is ups else m + 1, k)

        @pl.when(code)
        def _():
            for copy in coded(way, k, c):
                copy.wait_recv()
            decode(way[4], way[5], k, c)

        @pl.when(jnp.logical_not(code))
        def _():
            plain(way, k, c).wait_recv()
            piece = pl.ds(c * rows, rows)
            part[k, piece, :] += way[3][k, piece, :]

    span = tile_of(width)

    def product(position):
        k = target(position)
        load(position).wait()
        if position + 1 < M:
            load(position + 1).start()

        @pl.loop(0, width // span)
        def _(t):
            cols = pl.ds(pl.multiple_of(t * span, span), span)
            part[k, :, cols] = lax.dot_general(
                cot[...], wbuf[position % 2, cols, :],
                (((1,), (1,)), ((), ())), preferred_element_type=jnp.float32,
            )

        @pl.when((m == 0) & (k > m))
        def _():
            for c in range(CHUNKS):
                send_sum(ups, k, c)

        @pl.when((m == M - 1) & (k < m))
        def _():
            for c in range(CHUNKS):
                send_sum(downs, k, c)

    def arrivals(r):
        @pl.when(m >= r)
        def _():
            mm = m - r
            ctx_up(zctx.at[mm], mm).wait_recv()

            @pl.when(m < M - 1)
            def _():
                ctx_up(zctx.at[mm], mm).start()

            hand_out(zctx.at[mm], mm)

        @pl.when(m + r < M)
        def _():
            mm = m + r
            ctx_down(zctx.at[mm], mm).wait_recv()

            @pl.when(m > 0)
            def _():
                ctx_down(zctx.at[mm], mm).start()

            hand_out(zctx.at[mm], mm)

    def pass_on(way, k, c):
        take_sum(way, k, c)
        send_sum(way, k, c)

    def chain(tick):
        up = M - 1 - (tick - m)
        down = tick - (M - 1 - m)
        for c in range(CHUNKS):
            @pl.when((m > 0) & (m < up) & (up < M))
            def _():
                pass_on(ups, up, c)

            @pl.when((m < M - 1) & (m > down) & (down >= 0))
            def _():
                pass_on(downs, down, c)

    r = 1
    for position in range(M):
        product(position)
        if position % 2 == 1 and r < M:
            arrivals(r)
            r += 1
    if M > 2:
        chain(1)
    for dq in range(1, B * half):
        j = cot_from(dq)
        remote(cotall.at[j], cotall.at[j], kf.at[dq], kr.at[j], partner).wait_recv()
        cot_forward(dq).start()
    while r < M:
        arrivals(r)
        r += 1
    for tick in range(2, M - 1):
        chain(tick)

    own_cot.wait()
    for d in range(1, G):
        j = lax.rem(bs + d, G)
        remote(ctxall.at[j], ctxall.at[j], cs.at[j], cr.at[j], partner).wait_recv()
    pltpu.make_async_copy(ctxall.at[bs], ctxall.at[bs], cr.at[bs]).wait()
    remote(cotall.at[partner_bs], cotall.at[partner_bs], ks.at[0], kr.at[partner_bs], partner).wait_recv()
    for dq in range(1, B * half):
        j = cot_from(dq) + 1 - 2 * parity
        remote(cotall.at[j], cotall.at[j], kf.at[dq], kr.at[j], partner).wait_recv()

    for j in range(G):
        ctxt[:, j * T : (j + 1) * T] = ctxall[j].T
    gspan = tile_of(width)

    @pl.loop(0, width // gspan)
    def _(t):
        cols = pl.ds(pl.multiple_of(t * gspan, gspan), gspan)
        gw[:, cols] = jnp.dot(
            ctxt[...], cotall[:, :, cols].reshape(G * T, gspan),
            preferred_element_type=jnp.float32,
        )

    for c in range(CHUNKS):
        piece = pl.ds(c * rows, rows)

        @pl.when(m > 0)
        def _():
            take_sum(ups, m, c)

        @pl.when(m < M - 1)
        def _():
            take_sum(downs, m, c)

        gc[piece, :] = part[m, piece, :].astype(gc.dtype)

    for mm in range(M):
        @pl.when((m < M - 1) & (mm <= m))
        def _():
            ctx_up(ctx, mm).wait_send()

        @pl.when((m > 0) & (mm >= m))
        def _():
            ctx_down(ctx, mm).wait_send()

        for c in range(CHUNKS):
            @pl.when(mm > m)
            def _():
                sent_sum(ups, mm, c)

            @pl.when(mm < m)
            def _():
                sent_sum(downs, mm, c)

    for dest in range(G):
        @pl.when(dest != bs)
        def _():
            remote(piece_of(ctx, 0), ctxall.at[bs], cs.at[dest], cr.at[bs], partner).wait_send()

    cot_partner().wait_send()
    for dq in range(1, B * half):
        cot_send(dq).wait_send()
        cot_forward(dq).wait_send()


def shards(context, cotangent, out_weight):
    B, S, M = lax.axis_size("batch"), lax.axis_size("seq"), lax.axis_size("mp")
    G = B * S
    T, width = cotangent.shape
    Q = G // M
    F = context.shape[1] // Q
    pieces = context
    if F % 128:
        pieces = jnp.stack([context[:, h * F : (h + 1) * F] for h in range(Q)])
    pairs = B * (S // 2)
    dma = pltpu.SemaphoreType.DMA
    vmem = pl.BlockSpec(memory_space=pltpu.VMEM)
    return pl.pallas_call(
        functools.partial(kernel, B, S, M),
        out_shape=(
            jax.ShapeDtypeStruct((F, width), jnp.float32),
            jax.ShapeDtypeStruct((T, context.shape[1]), jnp.bfloat16),
        ),
        in_specs=[vmem, vmem, pl.BlockSpec(memory_space=pl.ANY)],
        out_specs=(vmem, vmem),
        scratch_shapes=[
            pltpu.VMEM((M, *pieces.shape), jnp.bfloat16),
            pltpu.VMEM((G, T, width), jnp.bfloat16),
            pltpu.VMEM((G, T, F), jnp.bfloat16),
            pltpu.VMEM((F, G * T), jnp.bfloat16),
            pltpu.VMEM((M, T, width), jnp.float32),
            pltpu.VMEM((M, T, width), jnp.float32),
            pltpu.VMEM((M, T, width), jnp.float32),
            pltpu.VMEM((M, T, width), jnp.bfloat16),
            pltpu.VMEM((M, T // PARTS, width), jnp.float32),
            pltpu.VMEM((M, T, width), jnp.bfloat16),
            pltpu.VMEM((M, T // PARTS, width), jnp.float32),
            pltpu.VMEM((M, T, width), jnp.bfloat16),
            pltpu.VMEM((M, T // PARTS, width), jnp.float32),
            pltpu.VMEM((2, width, width), jnp.bfloat16),
            dma((2,)), dma((M,)), dma((M,)), dma((M,)),
            dma((G,)), dma((G,)), dma((pairs,)), dma((pairs,)), dma((G,)),
            *[dma((M, CHUNKS, 2))] * 4,
        ],
        compiler_params=pltpu.CompilerParams(collective_id=0, has_side_effects=True, vmem_limit_bytes=46 * 1024 * 1024),
        name="output_projection_backward",
    )(pieces, cotangent, out_weight)


def solution(mesh):
    return jax.shard_map(
        shards,
        mesh=mesh,
        in_specs=(P(("batch", "seq"), "mp"), P(("batch", "seq"), "mp"), P(None, "mp")),
        out_specs=(P(("batch", "seq"), "mp"), P(("batch", "seq"), "mp")),
        check_vma=False,
    )
```

```python
import functools

import jax
import jax.numpy as jnp
from jax import lax
from jax.experimental import pallas as pl
from jax.experimental.pallas import tpu as pltpu
from jax.sharding import PartitionSpec as P

MESH = pl.DeviceIdType.MESH
CHUNKS = 2
PARTS = 4
LEVELS = 36
BASE = 75


def tile_of(width):
    return 256 if width % 256 == 0 else 128


def kernel(
    B, S, M,
    ctx, cot, w, gw, gc,
    zctx, cotall, ctxall, ctxt, part, rup, rdn, high, low_bits, hup, lup, hdn, ldn, wbuf,
    wsem, zr, zu, zd, cs, cr, ks, kf, kr, pus, pds, pur, pdr,
):
    G = B * S
    Q = G // M
    T, width = cot.shape
    rows = T // CHUNKS
    half = S // 2
    b, s, m = lax.axis_index("batch"), lax.axis_index("seq"), lax.axis_index("mp")
    bs = b * S + s
    parity = lax.rem(s, 2)
    partner = (b, s + 1 - 2 * parity, m)
    partner_bs = b * S + s + 1 - 2 * parity
    above, below = (b, s, m + 1), (b, s, m - 1)

    depth = ctxall.shape[2]

    def piece_of(ref, h):
        return ref.at[:, pl.ds(h * depth, depth)] if len(ctx.shape) == 2 else ref.at[h]

    def plane(index):
        return (index // S, lax.rem(index, S), m)

    def remote(src, dst, send, recv, device):
        return pltpu.make_async_remote_copy(
            src_ref=src, dst_ref=dst, send_sem=send, recv_sem=recv,
            device_id=device, device_id_type=MESH,
        )

    low = 2 * m < M

    def target(position):
        return jnp.where(low, M - 1 - position, position)

    def load(position):
        k = target(position)
        return pltpu.make_async_copy(
            w.at[pl.ds(k * width, width), :], wbuf.at[position % 2], wsem.at[position % 2]
        )

    load(0).start()
    own_cot = pltpu.make_async_copy(cot, cotall.at[bs], kr.at[bs])
    own_cot.start()

    barrier = pltpu.get_barrier_semaphore()
    for d in range(1, G):
        pl.semaphore_signal(
            barrier, inc=1, device_id=plane(lax.rem(bs + d, G)), device_id_type=MESH
        )

    @pl.when(m > 0)
    def _():
        pl.semaphore_signal(barrier, inc=1, device_id=below, device_id_type=MESH)

    @pl.when(m < M - 1)
    def _():
        pl.semaphore_signal(barrier, inc=1, device_id=above, device_id_type=MESH)

    edge = (m == 0) | (m == M - 1)

    @pl.when(edge)
    def _():
        pl.semaphore_wait(barrier, G)

    @pl.when(jnp.logical_not(edge))
    def _():
        pl.semaphore_wait(barrier, G + 1)

    def ctx_up(src, mm):
        return remote(src, zctx.at[mm], zu.at[mm], zr.at[mm], above)

    def ctx_down(src, mm):
        return remote(src, zctx.at[mm], zd.at[mm], zr.at[mm], below)

    def hand_out(src, mm):
        for h in range(Q):
            dest = mm * Q + h

            @pl.when(dest != bs)
            def _():
                remote(piece_of(src, h), ctxall.at[bs], cs.at[dest], cr.at[bs], plane(dest)).start()

            @pl.when(dest == bs)
            def _():
                pltpu.make_async_copy(piece_of(src, h), ctxall.at[bs], cr.at[bs]).start()

    @pl.when(m < M - 1)
    def _():
        ctx_up(ctx, m).start()

    @pl.when(m > 0)
    def _():
        ctx_down(ctx, m).start()

    def cot_send(dq):
        q = lax.rem(b * half + s // 2 + dq, B * half)
        dest = (q // half, lax.rem(q, half) * 2 + parity, m)
        return remote(cot, cotall.at[bs], ks.at[dq], kr.at[bs], dest)

    def cot_partner():
        return remote(cot, cotall.at[bs], ks.at[0], kr.at[bs], partner)

    def cot_from(dq):
        q = lax.rem(b * half + s // 2 + dq, B * half)
        return (q // half) * S + lax.rem(q, half) * 2 + parity

    def cot_forward(dq):
        j = cot_from(dq)
        return remote(cotall.at[j], cotall.at[j], kf.at[dq], kr.at[j], partner)

    cot_partner().start()
    for dq in range(1, B * half):
        cot_send(dq).start()
    hand_out(ctx, m)

    def chunk(ref, k, c):
        return ref.at[k, pl.ds(c * rows, rows), :]

    quarter = rows // PARTS
    ups = (above, pus, pur, rup, hup, lup)
    downs = (below, pds, pdr, rdn, hdn, ldn)

    def short(ref, k, c):
        return ref.at[k, pl.ds(c * quarter, quarter), :]

    def plain(way, k, c):
        device, send, recv, full, _, _ = way
        return remote(chunk(part, k, c), chunk(full, k, c), send.at[k, c, 0], recv.at[k, c, 0], device)

    def coded(way, k, c):
        device, send, recv, _, rhigh, rlow = way
        return (
            remote(chunk(high, k, c), chunk(rhigh, k, c), send.at[k, c, 0], recv.at[k, c, 0], device),
            remote(short(low_bits, k, c), short(rlow, k, c), send.at[k, c, 1], recv.at[k, c, 1], device),
        )

    def is_coded(way, sender):
        if way is ups:
            return (sender == 0) | (sender < M - 2)
        return (sender == M - 1) | (sender > 1)

    def encode(k, c):
        @pl.loop(0, width // span)
        def _(t):
            cols = pl.ds(pl.multiple_of(t * span, span), span)
            total = None
            for i in range(PARTS):
                lines = pl.ds(c * rows + i * quarter, quarter)
                value = part[k, lines, cols]
                top = value.astype(jnp.bfloat16)
                high[k, lines, cols] = top
                top = top.astype(jnp.float32)
                size = jnp.abs(top)
                usable = size > 1e-30
                scale = (256.0 * LEVELS) / jnp.where(usable, size, 1.0)
                rest = jnp.floor(jnp.where(usable, (value - top) * scale, 0.0) + 0.5)
                total = rest if total is None else total * BASE + rest
            low_bits[k, pl.ds(c * quarter, quarter), cols] = total

    def decode(rhigh, rlow, k, c):
        @pl.loop(0, width // span)
        def _(t):
            cols = pl.ds(pl.multiple_of(t * span, span), span)
            left = rlow[k, pl.ds(c * quarter, quarter), cols]
            for i in range(PARTS):
                lines = pl.ds(c * rows + i * quarter, quarter)
                unit = float(BASE ** (PARTS - 1 - i))
                rest = jnp.floor(left * (1.0 / unit) + 0.5)
                left = left - rest * unit
                top = rhigh[k, lines, cols].astype(jnp.float32)
                value = top + rest * (jnp.abs(top) * (1.0 / (256.0 * LEVELS)))
                part[k, lines, cols] += value

    def send_sum(way, k, c):
        code = is_coded(way, m)

        @pl.when(code)
        def _():
            encode(k, c)
            for copy in coded(way, k, c):
                copy.start()

        @pl.when(jnp.logical_not(code))
        def _():
            plain(way, k, c).start()

    def sent_sum(way, k, c):
        code = is_coded(way, m)

        @pl.when(code)
        def _():
            for copy in coded(way, k, c):
                copy.wait_send()

        @pl.when(jnp.logical_not(code))
        def _():
            plain(way, k, c).wait_send()

    def take_sum(way, k, c):
        code = is_coded(way, m - 1 if way is ups else m + 1)

        @pl.when(code)
        def _():
            for copy in coded(way, k, c):
                copy.wait_recv()
            decode(way[4], way[5], k, c)

        @pl.when(jnp.logical_not(code))
        def _():
            plain(way, k, c).wait_recv()
            piece = pl.ds(c * rows, rows)
            part[k, piece, :] += way[3][k, piece, :]

    span = tile_of(width)

    def product(position):
        k = target(position)
        load(position).wait()
        if position + 1 < M:
            load(position + 1).start()

        @pl.loop(0, width // span)
        def _(t):
            cols = pl.ds(pl.multiple_of(t * span, span), span)
            part[k, :, cols] = lax.dot_general(
                cotall[bs], wbuf[position % 2, cols, :],
                (((1,), (1,)), ((), ())), preferred_element_type=jnp.float32,
            )

        @pl.when((m == 0) & (k > m))
        def _():
            for c in range(CHUNKS):
                send_sum(ups, k, c)

        @pl.when((m == M - 1) & (k < m))
        def _():
            for c in range(CHUNKS):
                send_sum(downs, k, c)

    own_cot.wait()

    def arrivals(r):
        @pl.when(m >= r)
        def _():
            mm = m - r
            ctx_up(zctx.at[mm], mm).wait_recv()

            @pl.when(m < M - 1)
            def _():
                ctx_up(zctx.at[mm], mm).start()

            hand_out(zctx.at[mm], mm)

        @pl.when(m + r < M)
        def _():
            mm = m + r
            ctx_down(zctx.at[mm], mm).wait_recv()

            @pl.when(m > 0)
            def _():
                ctx_down(zctx.at[mm], mm).start()

            hand_out(zctx.at[mm], mm)

    def pass_on(way, k, c):
        take_sum(way, k, c)
        send_sum(way, k, c)

    def chain(tick):
        up = M - 1 - (tick - m)
        down = tick - (M - 1 - m)
        for c in range(CHUNKS):
            @pl.when((m > 0) & (m < up) & (up < M))
            def _():
                pass_on(ups, up, c)

            @pl.when((m < M - 1) & (m > down) & (down >= 0))
            def _():
                pass_on(downs, down, c)

    r = 1
    for position in range(M):
        product(position)
        if position % 2 == 1 and r < M:
            arrivals(r)
            r += 1
    if M > 2:
        chain(1)
    for dq in range(1, B * half):
        j = cot_from(dq)
        remote(cotall.at[j], cotall.at[j], kf.at[dq], kr.at[j], partner).wait_recv()
        cot_forward(dq).start()
    while r < M:
        arrivals(r)
        r += 1
    for tick in range(2, M - 1):
        chain(tick)

    for d in range(1, G):
        j = lax.rem(bs + d, G)
        remote(ctxall.at[j], ctxall.at[j], cs.at[j], cr.at[j], partner).wait_recv()
    pltpu.make_async_copy(ctxall.at[bs], ctxall.at[bs], cr.at[bs]).wait()
    remote(cotall.at[partner_bs], cotall.at[partner_bs], ks.at[0], kr.at[partner_bs], partner).wait_recv()
    for dq in range(1, B * half):
        j = cot_from(dq) + 1 - 2 * parity
        remote(cotall.at[j], cotall.at[j], kf.at[dq], kr.at[j], partner).wait_recv()

    for j in range(G):
        ctxt[:, j * T : (j + 1) * T] = ctxall[j].T
    gspan = tile_of(width)

    @pl.loop(0, width // gspan)
    def _(t):
        cols = pl.ds(pl.multiple_of(t * gspan, gspan), gspan)
        gw[:, cols] = jnp.dot(
            ctxt[...], cotall[:, :, cols].reshape(G * T, gspan),
            preferred_element_type=jnp.float32,
        )

    for c in range(CHUNKS):
        piece = pl.ds(c * rows, rows)

        @pl.when(m > 0)
        def _():
            take_sum(ups, m, c)

        @pl.when(m < M - 1)
        def _():
            take_sum(downs, m, c)

        gc[piece, :] = part[m, piece, :].astype(gc.dtype)

    for mm in range(M):
        @pl.when((m < M - 1) & (mm <= m))
        def _():
            ctx_up(ctx, mm).wait_send()

        @pl.when((m > 0) & (mm >= m))
        def _():
            ctx_down(ctx, mm).wait_send()

        for c in range(CHUNKS):
            @pl.when(mm > m)
            def _():
                sent_sum(ups, mm, c)

            @pl.when(mm < m)
            def _():
                sent_sum(downs, mm, c)

    for dest in range(G):
        @pl.when(dest != bs)
        def _():
            remote(piece_of(ctx, 0), ctxall.at[bs], cs.at[dest], cr.at[bs], partner).wait_send()

    cot_partner().wait_send()
    for dq in range(1, B * half):
        cot_send(dq).wait_send()
        cot_forward(dq).wait_send()


def shards(context, cotangent, out_weight):
    B, S, M = lax.axis_size("batch"), lax.axis_size("seq"), lax.axis_size("mp")
    G = B * S
    T, width = cotangent.shape
    Q = G // M
    F = context.shape[1] // Q
    pieces = context
    if F % 128:
        pieces = jnp.stack([context[:, h * F : (h + 1) * F] for h in range(Q)])
    pairs = B * (S // 2)
    dma = pltpu.SemaphoreType.DMA
    vmem = pl.BlockSpec(memory_space=pltpu.VMEM)
    hbm = pl.BlockSpec(memory_space=pltpu.HBM)
    return pl.pallas_call(
        functools.partial(kernel, B, S, M),
        out_shape=(
            jax.ShapeDtypeStruct((F, width), jnp.float32),
            jax.ShapeDtypeStruct((T, context.shape[1]), jnp.bfloat16),
        ),
        in_specs=[hbm, hbm, hbm],
        out_specs=(vmem, vmem),
        scratch_shapes=[
            pltpu.VMEM((M, *pieces.shape), jnp.bfloat16),
            pltpu.VMEM((G, T, width), jnp.bfloat16),
            pltpu.VMEM((G, T, F), jnp.bfloat16),
            pltpu.VMEM((F, G * T), jnp.bfloat16),
            pltpu.VMEM((M, T, width), jnp.float32),
            pltpu.VMEM((M, T, width), jnp.float32),
            pltpu.VMEM((M, T, width), jnp.float32),
            pltpu.VMEM((M, T, width), jnp.bfloat16),
            pltpu.VMEM((M, T // PARTS, width), jnp.float32),
            pltpu.VMEM((M, T, width), jnp.bfloat16),
            pltpu.VMEM((M, T // PARTS, width), jnp.float32),
            pltpu.VMEM((M, T, width), jnp.bfloat16),
            pltpu.VMEM((M, T // PARTS, width), jnp.float32),
            pltpu.VMEM((2, width, width), jnp.bfloat16),
            dma((2,)), dma((M,)), dma((M,)), dma((M,)),
            dma((G,)), dma((G,)), dma((pairs,)), dma((pairs,)), dma((G,)),
            *[dma((M, CHUNKS, 2))] * 4,
        ],
        compiler_params=pltpu.CompilerParams(collective_id=0, has_side_effects=True, vmem_limit_bytes=46 * 1024 * 1024),
        name="output_projection_backward",
    )(pieces, cotangent, out_weight)


def solution(mesh):
    return jax.shard_map(
        shards,
        mesh=mesh,
        in_specs=(P(("batch", "seq"), "mp"), P(("batch", "seq"), "mp"), P(None, "mp")),
        out_specs=(P(("batch", "seq"), "mp"), P(("batch", "seq"), "mp")),
        check_vma=False,
    )
```
